128 devices in a mesh: sample: 2 (over core), sx: 8 (over z_hi, y), sy: 8 (over x, z_lo).
Axes of the slice: x: 4, y: 4, z: 4 (z_hi: 2, z_lo: 2; z = z_hi * 2 + z_lo), core: 2. Of those that a mesh axis runs over, the one named last changes fastest.
Arguments:
- features: bfloat16 [32, 4, 32, 32, 256], P('sx', 'sample', 'sy'), may hold values from -6 to 6
- kernel: bfloat16 [3, 3, 3, 256, 256], P(None, None, None, 'sx', 'sy'), may hold values from -0.078125 to 0.078125
- filter_bias: bfloat16 [256], P('sy'), may hold values from -3 to 3
- cotangent: bfloat16 [32, 4, 32, 32, 256], P('sx', 'sample', None, None, 'sy'), may hold values from -6 to 6
Outputs:
- output: bfloat16 [32, 4, 32, 32, 256], P('sx', 'sample', None, None, 'sy')
- input_grad: bfloat16 [32, 4, 32, 32, 256], P('sx', 'sample', 'sy')
- kernel_grad: float32 [3, 3, 3, 256, 256], P(None, None, None, 'sx', 'sy')
The draws below stay inside these ranges and needn't reach their ends.
All inputs are finite; a program needn't handle non-finite values.
Results may differ from the reference program's by a relative error of at most 0.014.
Values may be sent and summed in bfloat16 or wider, within the bound.
No kernel may reach another device: no remote copies, remote signals or barrier semaphores. Data moves between devices by JAX's collectives and lax.ppermute only.
A program may use at most 128 MiB of HBM per device.

```python
import jax
import jax.numpy as jnp
from jax import lax

CH = 256
FILT = 256
DEPTH = 32
GX = 32
GY = 32
SAMPLES = 4


def block_scale(key, shape, split, smallest, largest):
    def one(axis_at, shards_of):
        steps = jax.random.uniform(jax.random.fold_in(jax.random.fold_in(key, 6), axis_at), (shards_of,), jnp.float32, smallest / len(split), largest / len(split))
        return jnp.repeat(jnp.exp(steps), shape[axis_at] // shards_of).reshape((-1,) + (1,) * (len(shape) - axis_at - 1))

    level = one(*split[0])
    for cut in split[1:]:
        level = level * one(*cut)
    return level


def bell_draw(key, shape, scale, limit, shards=(), dtype=jnp.bfloat16):
    array = scale * jax.random.normal(key, shape, jnp.float32)
    if shards:
        array = array * block_scale(key, shape, shards, -0.22, 0.18)
    return jnp.clip(array, -limit, limit).astype(dtype)


def setup_inputs(seed: int = 0) -> dict:
    splits = jax.random.split(jax.random.key(seed), 5)
    return {
        "features": bell_draw(splits[0], (GX, SAMPLES, GY, DEPTH, CH), 1.0, 6.0, ((0, 8), (1, 2), (2, 8))),
        "kernel": bell_draw(splits[1], (3, 3, 3, CH, FILT), (27 * CH) ** -0.5, 0.078125, ((3, 8), (4, 8))),
        "filter_bias": bell_draw(splits[2], (FILT,), 0.5, 3.0, ((0, 8),)),
        "cotangent": bell_draw(splits[3], (GX, SAMPLES, GY, DEPTH, FILT), 1.0, 6.0, ((0, 8), (1, 2), (4, 8))),
    }


def slope_of(hidden):
    gate = jax.nn.sigmoid(hidden)
    return gate * (1.0 + hidden * (1.0 - gate))


def window_of(padded, first, second, third, rows_x, rows_y, rows_z):
    piece = padded[first:first + rows_x, :, second:second + rows_y, third:third + rows_z, :]
    return piece.reshape(-1, piece.shape[-1])


def reference(features, kernel, filter_bias, cotangent):
    rows_x = features.shape[0]
    count = features.shape[1]
    rows_y = features.shape[2]
    rows_z = features.shape[3]
    channels = features.shape[4]
    filters = kernel.shape[4]
    padded = jnp.pad(features, ((1, 1), (0, 0), (1, 1), (1, 1), (0, 0)))
    hidden = jnp.zeros((rows_x * count * rows_y * rows_z, filters), jnp.float32)
    for first in range(3):
        for second in range(3):
            for third in range(3):
                window = window_of(padded, first, second, third, rows_x, rows_y, rows_z)
                hidden = hidden + jnp.dot(window, kernel[first, second, third], preferred_element_type=jnp.float32)
    hidden = hidden + filter_bias.astype(jnp.float32)[None, :]
    output = jax.nn.silu(hidden).astype(jnp.bfloat16).reshape(rows_x, count, rows_y, rows_z, filters)
    flat_cot = cotangent.reshape(-1, filters).astype(jnp.float32)
    grad_flat = (flat_cot * slope_of(hidden)).astype(jnp.bfloat16)
    grad_pre = grad_flat.reshape(rows_x, count, rows_y, rows_z, filters)
    grad_padded = jnp.pad(grad_pre, ((1, 1), (0, 0), (1, 1), (1, 1), (0, 0)))
    input_grad = jnp.zeros((rows_x * count * rows_y * rows_z, channels), jnp.float32)
    tap_grads = []
    for first in range(3):
        for second in range(3):
            for third in range(3):
                grad_window = window_of(grad_padded, 2 - first, 2 - second, 2 - third, rows_x, rows_y, rows_z)
                input_grad = input_grad + lax.dot_general(grad_window, kernel[first, second, third], (((1,), (1,)), ((), ())), preferred_element_type=jnp.float32)
                window = window_of(padded, first, second, third, rows_x, rows_y, rows_z)
                tap_grads.append(lax.dot_general(window, grad_flat, (((0,), (0,)), ((), ())), preferred_element_type=jnp.float32))
    input_grad = input_grad.astype(jnp.bfloat16).reshape(rows_x, count, rows_y, rows_z, channels)
    kernel_grad = jnp.stack(tap_grads).reshape(3, 3, 3, channels, filters).astype(jnp.float32)
    return output, input_grad, kernel_grad
```

```python
import jax
import jax.numpy as jnp
from jax import lax
from jax.experimental import pallas as pl
from jax.experimental.pallas import tpu as pltpu
from jax.sharding import PartitionSpec as P

HALF = 14
GRID = ("sx", "sy")
BF16 = jnp.bfloat16
F32 = jnp.float32


def halo(array, axis, dim):
    size, length = (lax.axis_size(axis), array.shape[dim])
    up = [(i, i + 1) for i in range(size - 1)]
    down = [(j, i) for i, j in up]
    last = lax.slice_in_dim(array, length - 1, length, axis=dim)
    leading = lax.slice_in_dim(array, 0, 1, axis=dim)
    return lax.ppermute(last, axis, up), lax.ppermute(leading, axis, down)


def padded(array, axis, dim):
    before, after = halo(array, axis, dim)
    return jnp.concatenate([before, array, after], axis=dim)


def swap_cores(array):
    return lax.ppermute(array, "sample", [(0, 1), (1, 0)])


def call(body, out, grid=None, ins=None, outs=None, scratch=(), limit=48):
    extra = {}
    if grid is not None:
        extra = {"grid": grid, "in_specs": ins, "out_specs": outs}
    elif ins is not None:
        extra = {"in_specs": ins}
    return pl.pallas_call(
        body,
        out_shape=out,
        scratch_shapes=list(scratch),
        compiler_params=pltpu.CompilerParams(vmem_limit_bytes=limit << 20),
        **extra,
    )


def shape(dims, dtype=BF16):
    return jax.ShapeDtypeStruct(dims, dtype)


def turn(parts):
    a = parts
    lane = lax.broadcasted_iota(jnp.int32, a[0].shape, 1)
    low = lane < 64
    even = (lane // 32) % 2 == 0

    def pair(x, y, mask, step):
        first = jnp.where(mask, x, pltpu.roll(y, step, 1))
        second = jnp.where(mask, pltpu.roll(x, 128 - step, 1), y)
        return first, second

    a0, a2 = pair(a[0], a[2], low, 64)
    a1, a3 = pair(a[1], a[3], low, 64)
    b0, b1 = pair(a0, a1, even, 32)
    b2, b3 = pair(a2, a3, even, 32)
    return [b0, b1, b2, b3]


def pack_kernel_body(core, taps, out):
    rows = []
    for t in range(HALF // 2):
        one = taps[core[0] * HALF + 2 * t].astype(F32)
        two = taps[core[0] * HALF + 2 * t + 1].astype(F32)
        rows.append(jnp.concatenate([one[:16], one[16:], two[:16], two[16:]], axis=1))
    block = jnp.concatenate(rows, axis=0).astype(BF16)
    out[...] = jnp.broadcast_to(block[None], out.shape)


def unpack_kernel_body(mine, out):
    for t in range(HALF // 2):
        for high in range(2):
            parts = [mine[high * 4 + s, 16 * t : 16 * t + 16, :] for s in range(4)]
            for g, part in enumerate(turn(parts)):
                rows = pl.ds(16 * (g % 2), 16)
                out[2 * t + g // 2, rows, 128 * high : 128 * high + 128] = part


def pack_grad_body(core, own, received, out):
    start = core[0] * 13
    for t in range(HALF // 2):
        for high in range(2):
            parts = []
            for g in range(4):
                slot, rows = 2 * t + g // 2, pl.ds(16 * (g % 2), 16)
                lanes = pl.ds(128 * high, 128)
                total = own[start + slot, rows, lanes].astype(F32) + received[slot, rows, lanes].astype(F32)
                parts.append(total.astype(BF16))
            for s, part in enumerate(turn(parts)):
                out[high * 4 + s, 0, 16 * t : 16 * t + 16, :] = part


def sum_grad_body(blocks, out):
    total = blocks[0].astype(F32)
    for n in range(1, 64):
        total = total + blocks[n].astype(F32)
    out[...] = total


def unpack_grad_body(core, mine, other, out):
    zero = core[0] == 0
    first = jnp.where(zero, mine[...], other[...])
    second = jnp.where(zero, other[...], mine[...])
    for start, source in ((0, first), (13, second)):
        for t in range(HALF // 2):
            rows = source[16 * t : 16 * t + 16]
            for u in range(2):
                piece = jnp.concatenate([rows[:, 64 * u : 64 * u + 32], rows[:, 64 * u + 32 : 64 * u + 64]], axis=0)
                out[start + 2 * t + u] = piece.T


def pack_cotangent_body(cot, out):
    for s in range(2):
        parts = [cot[p, s].reshape(1024, 32).astype(F32) for p in range(4)]
        block = jnp.concatenate(parts, axis=1).astype(BF16)
        out[:, 128 * s : 128 * s + 128, :] = block.reshape(8, 128, 128)


def unpack_output_body(block, out):
    for s in range(2):
        rows = block[:, 128 * s : 128 * s + 128, :].reshape(1024, 128).astype(F32)
        for p in range(4):
            out[p, s] = rows[:, 32 * p : 32 * p + 32].reshape(32, 32, 32).astype(BF16)


def fill_shifts(source, target):
    row = lax.broadcasted_iota(jnp.int32, (192, 256), 0) % 32

    def plane(n, carry):
        a, s = n // 2, n % 2
        x = source[a, s]
        wide = x.astype(F32)
        before = jnp.where(row == 0, 0.0, pltpu.roll(wide, 1, 0))
        after = jnp.where(row == 31, 0.0, pltpu.roll(wide, 191, 0))
        target[a, s, :, 0:256] = before.astype(BF16)
        target[a, s, :, 256:512] = x
        target[a, s, :, 512:768] = after.astype(BF16)
        return carry

    lax.fori_loop(0, 12, plane, 0)


def by_core(core, run, mine, other):
    @pl.when(core[0] == 0)
    def _():
        run(mine, other)

    @pl.when(core[0] == 1)
    def _():
        run(other, mine)


def forward_body(core, window, mine, other, cot, shifts, grad_pre, packed, cots, outs):
    fill_shifts(window, shifts)
    for high in range(2):
        parts = turn([cot[high * 4 + s] for s in range(4)])
        for p in range(4):
            cots[p, :, 128 * high : 128 * high + 128] = parts[p]

    def run(first, second):
        bias = second[13, 0:1, :].astype(F32)

        def plane(p, carry):
            total = jnp.zeros((256, 256), F32)
            for i in range(3):
                for j in range(3):
                    start = 9 * i + 3 * j
                    source = first if start < HALF else second
                    at = start % HALF
                    count = min(3, HALF - at)
                    lhs = shifts[p + i, :, 32 * j : 32 * j + 128, 0 : 256 * count].reshape(256, 256 * count)
                    rhs = source[at : at + count].reshape(256 * count, 256)
                    total = total + jnp.dot(lhs, rhs, preferred_element_type=F32)
                    if count < 3:
                        lhs = shifts[p + i, :, 32 * j : 32 * j + 128, 256 * count : 768].reshape(256, 768 - 256 * count)
                        rhs = second[0 : 3 - count].reshape(768 - 256 * count, 256)
                        total = total + jnp.dot(lhs, rhs, preferred_element_type=F32)
            hidden = total + bias
            gate = 1.0 / (1.0 + jnp.exp(-hidden))
            outs[p] = (hidden * gate).astype(BF16)
            slope = gate * (1.0 + hidden * (1.0 - gate))
            grad_pre[p] = (cots[p].astype(F32) * slope).astype(BF16).reshape(2, 128, 256)
            return carry

        lax.fori_loop(0, 4, plane, 0)

    by_core(core, run, mine, other)
    for high in range(2):
        parts = turn([outs[p, :, 128 * high : 128 * high + 128] for p in range(4)])
        for s in range(4):
            packed[high * 4 + s] = parts[s]


def kernel_grad_body(shifts, grad_pre, out, turned):
    for p in range(4):
        turned[:, 256 * p : 256 * p + 256] = grad_pre[p].reshape(256, 256).astype(F32).T.astype(BF16)
    lhs = turned[...]
    for i in range(3):
        for j in range(3):
            rhs = shifts[i : i + 4, :, 32 * j : 32 * j + 128, :].reshape(1024, 768)
            res = jnp.dot(lhs, rhs, preferred_element_type=F32).astype(BF16)
            for k in range(3):
                out[9 * i + 3 * j + k] = res[:, 256 * k : 256 * k + 256]


def input_grad_body(core, window, mine, other, out, shifts):
    fill_shifts(window, shifts)

    def run(first, second):
        def plane(p, carry):
            total = jnp.zeros((256, 256), F32)
            for i in range(3):
                for j in range(3):
                    for k in range(3):
                        tap = 9 * i + 3 * j + k
                        rhs = first[tap] if tap < HALF else second[tap - HALF]
                        lanes = pl.ds(256 * (2 - k), 256)
                        lhs = shifts[p + 2 - i, :, 32 * (2 - j) : 32 * (2 - j) + 128, lanes].reshape(256, 256)
                        total = total + lax.dot_general(
                            lhs, rhs, (((1,), (1,)), ((), ())), preferred_element_type=F32
                        )
            out[p] = total.astype(BF16).reshape(2, 128, 256)
            return carry

        lax.fori_loop(0, 4, plane, 0)

    by_core(core, run, mine, other)


SMEM = pl.BlockSpec(memory_space=pltpu.SMEM)
FULL = pl.BlockSpec(memory_space=pltpu.VMEM)


def local(features, kernel, filter_bias, cotangent):
    core = lax.axis_index("sample").astype(jnp.int32)
    index = core[None]
    bias = jnp.broadcast_to(filter_bias[None, None, :], (1, 32, 32))
    taps = jnp.concatenate([kernel.reshape(27, 32, 32), bias], axis=0)
    blocks = call(pack_kernel_body, shape((64, 112, 128)), ins=[SMEM, FULL])(index, taps)
    blocks = lax.all_to_all(blocks, GRID, 0, 0, tiled=True)
    before, after = halo(features, "sx", 0)
    cot = call(pack_cotangent_body, shape((8, 256, 128)))(cotangent)
    before, after, blocks, cot = lax.optimization_barrier((before, after, blocks, cot))
    window = jnp.concatenate([before, features, after], axis=0)
    cot = lax.all_to_all(cot, "sy", 0, 0, tiled=True)
    window = padded(window, "sy", 2).reshape(6, 2, 192, 256)
    mine = call(
        unpack_kernel_body,
        shape((HALF, 256, 256)),
        (8,),
        [pl.BlockSpec((8, 112, 128), lambda n: (n, 0, 0))],
        pl.BlockSpec((HALF, 32, 256), lambda n: (0, n, 0)),
    )(blocks)
    other = swap_cores(mine)
    shifts, grad_pre, packed = call(
        forward_body,
        (shape((6, 2, 192, 768)), shape((4, 2, 128, 256)), shape((8, 256, 128))),
        ins=[SMEM, FULL, FULL, FULL, FULL],
        scratch=[pltpu.VMEM((4, 256, 256), BF16), pltpu.VMEM((4, 256, 256), BF16)],
    )(index, window, mine, other, cot)
    packed = lax.all_to_all(packed, "sy", 0, 0, tiled=True)
    grad_window = padded(grad_pre.reshape(4, 2, 4, 32, 256), "sx", 0)
    local_grad = call(kernel_grad_body, shape((27, 256, 256)), scratch=[pltpu.VMEM((256, 1024), BF16)])(
        shifts, grad_pre
    )
    received = swap_cores(lax.dynamic_slice_in_dim(local_grad, (1 - core) * 13, HALF, axis=0))
    grad_window = padded(grad_window, "sy", 2).reshape(6, 2, 192, 256)
    blocks = call(
        pack_grad_body,
        shape((8, 8, 112, 128)),
        (8,),
        [
            SMEM,
            pl.BlockSpec((27, 32, 256), lambda n: (0, n, 0)),
            pl.BlockSpec((HALF, 32, 256), lambda n: (0, n, 0)),
        ],
        pl.BlockSpec((8, 1, 112, 128), lambda n: (0, n, 0, 0)),
    )(index, local_grad, received)
    blocks, packed = lax.optimization_barrier((blocks, packed))
    blocks = lax.all_to_all(blocks.reshape(64, 112, 128), GRID, 0, 0, tiled=True)
    input_grad = call(
        input_grad_body,
        shape((4, 2, 128, 256)),
        ins=[SMEM, FULL, FULL, FULL],
        scratch=[pltpu.VMEM((6, 2, 192, 768), BF16)],
    )(index, grad_window, mine, other)
    output = call(unpack_output_body, shape((4, 2, 32, 32, 32)))(packed)
    blocks, input_grad, output = lax.optimization_barrier((blocks, input_grad, output))
    rows = call(sum_grad_body, shape((112, 128), F32))(blocks)
    kernel_grad = call(unpack_grad_body, shape((27, 32, 32), F32), ins=[SMEM, FULL, FULL])(
        index, rows, swap_cores(rows)
    )
    return (output, input_grad.reshape(4, 2, 4, 32, 256), kernel_grad.reshape(3, 3, 3, 32, 32))


def solution(mesh):
    return jax.shard_map(
        local,
        mesh=mesh,
        in_specs=(
            P("sx", "sample", "sy", None, None),
            P(None, None, None, "sx", "sy"),
            P("sy"),
            P("sx", "sample", None, None, "sy"),
        ),
        out_specs=(
            P("sx", "sample", None, None, "sy"),
            P("sx", "sample", "sy", None, None),
            P(None, None, None, "sx", "sy"),
        ),
        check_vma=False,
    )
```

```python
import jax
import jax.numpy as jnp
from jax import lax
from jax.experimental import pallas as pl
from jax.experimental.pallas import tpu as pltpu
from jax.sharding import PartitionSpec as P

HALF = 14
GRID = ("sx", "sy")
BF16 = jnp.bfloat16
F32 = jnp.float32


def halo(array, axis, dim):
    size, length = (lax.axis_size(axis), array.shape[dim])
    up = [(i, i + 1) for i in range(size - 1)]
    down = [(j, i) for i, j in up]
    last = lax.slice_in_dim(array, length - 1, length, axis=dim)
    leading = lax.slice_in_dim(array, 0, 1, axis=dim)
    return lax.ppermute(last, axis, up), lax.ppermute(leading, axis, down)


def corners(before, array, after):
    edge = shape((6, 2, 1, 32, 256))
    leading, last = call(edges_body, (edge, edge))(before, array, after)
    up = [(i, i + 1) for i in range(7)]
    down = [(j, i) for i, j in up]
    return lax.ppermute(last, "sy", up), lax.ppermute(leading, "sy", down)


def swap_cores(array):
    return lax.ppermute(array, "sample", [(0, 1), (1, 0)])


def swap_sides(array):
    return lax.ppermute(array, "sy", [(i, i + 1 - 2 * (i % 2)) for i in range(8)])


def spread(own, got):
    pieces = call(join_body, tuple(shape((2, 256, 128)) for _ in range(4)))(own, got)
    moved = [
        lax.ppermute(pieces[d], "sy", [(i, (i // 2 + d) % 4 * 2 + i % 2) for i in range(8)]) for d in range(1, 4)
    ]
    return [pieces[0], *moved]


def padded_bytes(x):
    dims = [1, *x.shape]
    lanes, rows = -(-dims[-1] // 128) * 128, -(-dims[-2] // 16) * 16
    size = lanes * rows * jnp.dtype(x.dtype).itemsize
    for dim in dims[:-2]:
        size *= dim
    return size


def call(body, out, scratch=(), far=(), far_out=()):
    outs = list(out) if isinstance(out, tuple) else [out]

    def run(*args):
        scalars = [x.dtype == jnp.int32 for x in args]
        held = list(far)
        written = list(far_out)

        def kernel(*refs):
            count = len(args) + len(outs)
            near = list(refs[:count])
            extra = refs[count:]
            sems = extra[-1]
            copies = []
            for at, n in enumerate(held):
                near[n] = extra[at]
                copies.append(pltpu.make_async_copy(refs[n], near[n], sems.at[at]))
            for copy in copies:
                copy.start()
            for at, n in enumerate(written):
                near[len(args) + n] = extra[len(held) + at]
            for copy in copies:
                copy.wait()
            body(*near, *extra[len(held) + len(written) : -1])
            copies = []
            for at, n in enumerate(written):
                to = refs[len(args) + n]
                copies.append(pltpu.make_async_copy(near[len(args) + n], to, sems.at[len(held) + at]))
            for copy in copies:
                copy.start()
            for copy in copies:
                copy.wait()

        rooms = [pltpu.VMEM(args[n].shape, args[n].dtype) for n in held]
        rooms += [pltpu.VMEM(outs[n].shape, outs[n].dtype) for n in written]
        rooms += list(scratch)
        total = sum(padded_bytes(x) for x in rooms)
        total += sum(padded_bytes(x) for n, x in enumerate(args) if n not in far)
        total += sum(padded_bytes(x) for n, x in enumerate(outs) if n not in far_out)
        specs = [SMEM if scalars[n] else FAR if n in far else FULL for n in range(len(args))]
        result = pl.pallas_call(
            kernel,
            out_shape=[pltpu.HBM(x.shape, x.dtype) if n in far_out else x for n, x in enumerate(outs)],
            in_specs=specs,
            out_specs=[FAR if n in far_out else FULL for n in range(len(outs))],
            scratch_shapes=[*rooms, pltpu.SemaphoreType.DMA((len(held) + len(written) + 1,))],
            compiler_params=pltpu.CompilerParams(vmem_limit_bytes=total + (3 << 20)),
        )(*[pltpu.with_memory_space_constraint(x, pltpu.HBM) if n in held else x for n, x in enumerate(args)])
        return result if isinstance(out, tuple) else result[0]

    return run


def shape(dims, dtype=BF16):
    return jax.ShapeDtypeStruct(dims, dtype)


def turn(parts):
    a = parts
    lane = lax.broadcasted_iota(jnp.int32, a[0].shape, 1)
    low = lane < 64
    even = (lane // 32) % 2 == 0

    def pair(x, y, mask, step):
        first = jnp.where(mask, x, pltpu.roll(y, step, 1))
        second = jnp.where(mask, pltpu.roll(x, 128 - step, 1), y)
        return first, second

    a0, a2 = pair(a[0], a[2], low, 64)
    a1, a3 = pair(a[1], a[3], low, 64)
    b0, b1 = pair(a0, a1, even, 32)
    b2, b3 = pair(a2, a3, even, 32)
    return [b0, b1, b2, b3]


def pack_kernel_body(core, taps, out):
    rows = []
    for t in range(HALF // 2):
        one = taps[core[0] * HALF + 2 * t].astype(F32)
        two = taps[core[0] * HALF + 2 * t + 1].astype(F32)
        rows.append(jnp.concatenate([one[:16], one[16:], two[:16], two[16:]], axis=1))
    block = jnp.concatenate(rows, axis=0).astype(BF16)
    out[...] = jnp.broadcast_to(block[None], out.shape)


def unpack_kernel_body(mine, out):
    def step(n, carry):
        for t in range(HALF // 2):
            for high in range(2):
                parts = [mine[8 * n + high * 4 + s, 16 * t : 16 * t + 16, :] for s in range(4)]
                for g, part in enumerate(turn(parts)):
                    rows = pl.ds(32 * n + 16 * (g % 2), 16)
                    out[2 * t + g // 2, rows, 128 * high : 128 * high + 128] = part
        return carry

    lax.fori_loop(0, 8, step, 0)


def pack_grad_body(kept, received, out):
    def step(n, carry):
        for t in range(HALF // 2):
            for high in range(2):
                parts = []
                for g in range(4):
                    slot, rows = 2 * t + g // 2, pl.ds(32 * n + 16 * (g % 2), 16)
                    lanes = pl.ds(128 * high, 128)
                    total = kept[slot, rows, lanes].astype(F32) + received[slot, rows, lanes].astype(F32)
                    parts.append(total.astype(BF16))
                for s, part in enumerate(turn(parts)):
                    out[8 * (high * 4 + s) + n, 16 * t : 16 * t + 16, :] = part
        return carry

    lax.fori_loop(0, 8, step, 0)


def sum_grad_body(blocks, out):
    total = blocks[0].astype(F32)
    for n in range(1, 64):
        total = total + blocks[n].astype(F32)
    out[...] = total


def unpack_grad_body(core, mine, other, out):
    zero = core[0] == 0
    first = jnp.where(zero, mine[...], other[...])
    second = jnp.where(zero, other[...], mine[...])
    for start, source in ((0, first), (13, second)):
        for t in range(HALF // 2):
            rows = source[16 * t : 16 * t + 16]
            for u in range(2):
                piece = jnp.concatenate([rows[:, 64 * u : 64 * u + 32], rows[:, 64 * u + 32 : 64 * u + 64]], axis=0)
                out[start + 2 * t + u] = piece.T


def blocks_of(place, turn_by, d):
    x, z = place[0] // 2, place[0] % 2
    column = (x + 4 + turn_by * d) % 4 * 2
    return column + z, column + 1 - z


def pack_cotangent_body(place, cot, keep, send):
    for d in range(4):
        for out, at in zip((keep, send), blocks_of(place, 1, d)):
            for s in range(2):
                parts = [cot[p, s, pl.ds(at * 4, 4)].reshape(128, 32).astype(F32) for p in range(4)]
                out[d, 128 * s : 128 * s + 128, :] = jnp.concatenate(parts, axis=1).astype(BF16)


def join_body(own, got, *outs):
    for d in range(4):
        outs[d][0] = own[d]
        outs[d][1] = got[d]


def unpack_output_body(place, *refs):
    out = refs[4]
    for d in range(4):
        for n, at in enumerate(blocks_of(place, -1, d)):
            for s in range(2):
                rows = refs[d][n, 128 * s : 128 * s + 128, :].astype(F32)
                for p in range(4):
                    out[p, s, pl.ds(at * 4, 4)] = rows[:, 32 * p : 32 * p + 32].reshape(4, 32, 32).astype(BF16)


def fill_shifts(pieces, target, window):
    middle, before, after, left, right = pieces
    window[0, :, 32:160, :] = before[0].reshape(2, 128, 256)
    window[1:5, :, 32:160, :] = middle[...].reshape(4, 2, 128, 256)
    window[5, :, 32:160, :] = after[0].reshape(2, 128, 256)
    window[:, :, 0:32, :] = left[...].reshape(6, 2, 32, 256)
    window[:, :, 160:192, :] = right[...].reshape(6, 2, 32, 256)
    row = lax.broadcasted_iota(jnp.int32, (192, 256), 0) % 32

    def plane(n, carry):
        a, s = n // 2, n % 2
        x = window[a, s]
        wide = x.astype(F32)
        up = jnp.where(row == 0, 0.0, pltpu.roll(wide, 1, 0))
        down = jnp.where(row == 31, 0.0, pltpu.roll(wide, 191, 0))
        target[a, s, :, 0:256] = up.astype(BF16)
        target[a, s, :, 256:512] = x
        target[a, s, :, 512:768] = down.astype(BF16)
        return carry

    lax.fori_loop(0, 12, plane, 0)


def by_core(core, run, swap=0):
    @pl.when(core[0] == swap)
    def _():
        run(0)

    @pl.when(core[0] == 1 - swap)
    def _():
        run(1)


def edges_body(before, array, after, leading, last):
    for out, at in ((leading, 0), (last, 3)):
        out[0, :, 0] = before[0, :, at]
        out[1:5, :, 0] = array[:, :, at]
        out[5, :, 0] = after[0, :, at]


def prepare_body(middle, before, after, left, right, shifts, window):
    fill_shifts((middle, before, after, left, right), shifts, window)


def groups_of(half):
    groups = []
    for tap in range(HALF * half, min(27, HALF * half + HALF)):
        i, j, k = tap // 9, tap // 3 % 3, tap % 3
        if groups and groups[-1][:2] == (i, j):
            groups[-1] = (i, j, groups[-1][2], groups[-1][3] + 1, groups[-1][4])
        else:
            groups.append((i, j, k, 1, tap - HALF * half))
    return groups


def conv_rows(shifts, weights, p, half):
    total = None
    for i, j, k, count, slot in groups_of(half):
        lanes = pl.ds(256 * k, 256 * count)
        lhs = shifts[p + i, :, 32 * j : 32 * j + 128, lanes].reshape(256, 256 * count)
        rhs = weights[slot : slot + count].reshape(256 * count, 256)
        term = jnp.dot(lhs, rhs, preferred_element_type=F32)
        total = term if total is None else total + term
    if half:
        total = total + weights[13, 0:1, :].astype(F32)
    return total


def forward_first_body(core, shifts, mine, partial):
    def run(half):
        def plane(p, carry):
            partial[p] = conv_rows(shifts, mine, p, half)
            return carry

        lax.fori_loop(0, 4, plane, 0)

    by_core(core, run)


def forward_second_body(core, place, shifts, other, partial, r0, r1, r2, r3, grad_pre, keep, send, blocks, cots, outs):
    for d, block in enumerate((r0, r1, r2, r3)):
        for n, at in enumerate(blocks_of(place, -1, d)):
            blocks[at] = block[n]
    for high in range(2):
        parts = turn([blocks[high * 4 + n] for n in range(4)])
        for p in range(4):
            cots[p, :, 128 * high : 128 * high + 128] = parts[p]

    def run(half):
        def plane(p, carry):
            hidden = partial[p] + conv_rows(shifts, other, p, half)
            gate = 1.0 / (1.0 + jnp.exp(-hidden))
            outs[p] = (hidden * gate).astype(BF16)
            slope = gate * (1.0 + hidden * (1.0 - gate))
            grad_pre[p] = (cots[p].astype(F32) * slope).astype(BF16).reshape(2, 4, 32, 256)
            return carry

        lax.fori_loop(0, 4, plane, 0)

    by_core(core, run, 1)
    for high in range(2):
        parts = turn([outs[p, :, 128 * high : 128 * high + 128] for p in range(4)])
        for n in range(4):
            blocks[high * 4 + n] = parts[n]
    for d in range(4):
        for out, at in zip((keep, send), blocks_of(place, 1, d)):
            out[d] = blocks[at]


def tap_grads(shifts, turned, out, half):
    for i in range(3):
        for j in range(3):
            taps = [k for k in range(3) if 13 * half <= 9 * i + 3 * j + k < 13 * half + HALF]
            if taps:
                lanes = pl.ds(256 * taps[0], 256 * len(taps))
                rhs = shifts[i : i + 4, :, 32 * j : 32 * j + 128, lanes].reshape(1024, 256 * len(taps))
                res = jnp.dot(turned[...], rhs, preferred_element_type=F32).astype(BF16)
                for n, k in enumerate(taps):
                    out[9 * i + 3 * j + k - 13 * half] = res[:, 256 * n : 256 * n + 256]


def give_grads_body(core, shifts, grad_pre, out, turned):
    for p in range(4):
        turned[:, 256 * p : 256 * p + 256] = grad_pre[p].reshape(256, 256).astype(F32).T.astype(BF16)
    by_core(core, lambda half: tap_grads(shifts, turned, out, half), 1)


def keep_grads_body(core, shifts, turned, out):
    by_core(core, lambda half: tap_grads(shifts, turned, out, half))


def input_grad_body(core, middle, before, after, left, right, mine, other, out, shifts, window):
    fill_shifts((middle, before, after, left, right), shifts, window)

    def run(half):
        first, second = (other, mine) if half else (mine, other)

        def plane(p, carry):
            total = jnp.zeros((256, 256), F32)
            for i in range(3):
                for j in range(3):
                    for k in range(3):
                        tap = 9 * i + 3 * j + k
                        rhs = first[tap] if tap < HALF else second[tap - HALF]
                        lanes = pl.ds(256 * (2 - k), 256)
                        lhs = shifts[p + 2 - i, :, 32 * (2 - j) : 32 * (2 - j) + 128, lanes].reshape(256, 256)
                        total = total + lax.dot_general(
                            lhs, rhs, (((1,), (1,)), ((), ())), preferred_element_type=F32
                        )
            out[p] = total.astype(BF16).reshape(2, 128, 256)
            return carry

        lax.fori_loop(0, 4, plane, 0)

    by_core(core, run)


SMEM = pl.BlockSpec(memory_space=pltpu.SMEM)
FULL = pl.BlockSpec(memory_space=pltpu.VMEM)
FAR = pl.BlockSpec(memory_space=pltpu.HBM)


def local(features, kernel, filter_bias, cotangent):
    core = lax.axis_index("sample").astype(jnp.int32)
    index = core[None]
    bias = jnp.broadcast_to(filter_bias[None, None, :], (1, 32, 32))
    taps = jnp.concatenate([kernel.reshape(27, 32, 32), bias], axis=0)
    place = lax.axis_index("sy").astype(jnp.int32)[None]
    four = shape((4, 256, 128))
    blocks = call(pack_kernel_body, shape((64, 112, 128)), far_out=(0,))(index, taps)
    keep, send = call(pack_cotangent_body, (four, four))(place, cotangent)
    before, after = halo(features, "sx", 0)
    got = swap_sides(send)
    blocks = lax.all_to_all(blocks, GRID, 0, 0, tiled=True)
    before, after, blocks, got = lax.optimization_barrier((before, after, blocks, got))
    left, right = corners(before, features, after)
    cot = spread(keep, got)
    mine = call(unpack_kernel_body, shape((HALF, 256, 256)), far=(0,))(blocks)
    other = swap_cores(mine)
    shifts = call(prepare_body, shape((6, 2, 192, 768)), [pltpu.VMEM((6, 2, 192, 256), BF16)])(
        features, before, after, left, right
    )
    planes = shape((4, 256, 256), F32)
    partial = call(forward_first_body, planes)(index, shifts, mine)
    grad_pre, keep, send = call(
        forward_second_body,
        (shape((4, 2, 4, 32, 256)), four, four),
        [pltpu.VMEM((8, 256, 128), BF16), pltpu.VMEM((4, 256, 256), BF16), pltpu.VMEM((4, 256, 256), BF16)],
    )(index, place, shifts, other, partial, *cot)
    before, after = halo(grad_pre, "sx", 0)
    got = swap_sides(send)
    given, turned = call(give_grads_body, (shape((HALF, 256, 256)), shape((256, 1024))))(index, shifts, grad_pre)
    given, before, after, got = lax.optimization_barrier((given, before, after, got))
    received = swap_cores(given)
    left, right = corners(before, grad_pre, after)
    kept = call(keep_grads_body, shape((HALF, 256, 256)))(index, shifts, turned)
    blocks = call(pack_grad_body, shape((64, 112, 128)), far_out=(0,))(kept, received)
    blocks, left, right, keep, got = lax.optimization_barrier((blocks, left, right, keep, got))
    blocks = lax.all_to_all(blocks, GRID, 0, 0, tiled=True)
    pieces = spread(keep, got)
    input_grad = call(
        input_grad_body,
        shape((4, 2, 128, 256)),
        [pltpu.VMEM((6, 2, 192, 768), BF16), pltpu.VMEM((6, 2, 192, 256), BF16)],
        far=(1, 2, 3, 4, 5, 6, 7),
    )(index, grad_pre, before, after, left, right, mine, other)
    blocks, input_grad = lax.optimization_barrier((blocks, input_grad))
    rows = call(sum_grad_body, shape((112, 128), F32))(blocks)
    kernel_grad = call(unpack_grad_body, shape((27, 32, 32), F32))(index, rows, swap_cores(rows))
    output = call(unpack_output_body, shape((4, 2, 32, 32, 32)))(place, *pieces)
    return (output, input_grad.reshape(4, 2, 4, 32, 256), kernel_grad.reshape(3, 3, 3, 32, 32))


def solution(mesh):
    return jax.shard_map(
        local,
        mesh=mesh,
        in_specs=(
            P("sx", "sample", "sy", None, None),
            P(None, None, None, "sx", "sy"),
            P("sy"),
            P("sx", "sample", None, None, "sy"),
        ),
        out_specs=(
            P("sx", "sample", None, None, "sy"),
            P("sx", "sample", "sy", None, None),
            P(None, None, None, "sx", "sy"),
        ),
        check_vma=False,
    )
```

```python
import jax
import jax.numpy as jnp
from jax import lax
from jax.experimental import pallas as pl
from jax.experimental.pallas import tpu as pltpu
from jax.sharding import PartitionSpec as P

HALF = 14
GRID = ("sx", "sy")
BF16 = jnp.bfloat16
F32 = jnp.float32


def halo(array, axis, dim):
    size, length = (lax.axis_size(axis), array.shape[dim])
    up = [(i, i + 1) for i in range(size - 1)]
    down = [(j, i) for i, j in up]
    last = lax.slice_in_dim(array, length - 1, length, axis=dim)
    leading = lax.slice_in_dim(array, 0, 1, axis=dim)
    return lax.ppermute(last, axis, up), lax.ppermute(leading, axis, down)


def corners(before, array, after):
    edge = shape((6, 2, 1, 32, 256))
    leading, last = call(edges_body, (edge, edge))(before, array, after)
    up = [(i, i + 1) for i in range(7)]
    down = [(j, i) for i, j in up]
    return lax.ppermute(last, "sy", up), lax.ppermute(leading, "sy", down)


def swap_cores(array):
    return lax.ppermute(array, "sample", [(0, 1), (1, 0)])


def swap_sides(array):
    return lax.ppermute(array, "sy", [(i, i + 1 - 2 * (i % 2)) for i in range(8)])


def spread(own, got):
    pieces = call(join_body, tuple(shape((2, 256, 128)) for _ in range(4)))(own, got)
    moved = [
        lax.ppermute(pieces[d], "sy", [(i, (i // 2 + d) % 4 * 2 + i % 2) for i in range(8)]) for d in range(1, 4)
    ]
    return [pieces[0], *moved]


def padded_bytes(x):
    dims = [1, *x.shape]
    lanes, rows = -(-dims[-1] // 128) * 128, -(-dims[-2] // 16) * 16
    size = lanes * rows * jnp.dtype(x.dtype).itemsize
    for dim in dims[:-2]:
        size *= dim
    return size


def call(body, out, scratch=(), far=(), far_out=()):
    outs = list(out) if isinstance(out, tuple) else [out]

    def run(*args):
        scalars = [x.dtype == jnp.int32 for x in args]
        held = list(far)
        written = list(far_out)

        def kernel(*refs):
            count = len(args) + len(outs)
            near = list(refs[:count])
            extra = refs[count:]
            sems = extra[-1]
            copies = []
            for at, n in enumerate(held):
                near[n] = extra[at]
                copies.append(pltpu.make_async_copy(refs[n], near[n], sems.at[at]))
            for copy in copies:
                copy.start()
            for at, n in enumerate(written):
                near[len(args) + n] = extra[len(held) + at]
            for copy in copies:
                copy.wait()
            body(*near, *extra[len(held) + len(written) : -1])
            copies = []
            for at, n in enumerate(written):
                to = refs[len(args) + n]
                copies.append(pltpu.make_async_copy(near[len(args) + n], to, sems.at[len(held) + at]))
            for copy in copies:
                copy.start()
            for copy in copies:
                copy.wait()

        rooms = [pltpu.VMEM(args[n].shape, args[n].dtype) for n in held]
        rooms += [pltpu.VMEM(outs[n].shape, outs[n].dtype) for n in written]
        rooms += list(scratch)
        total = sum(padded_bytes(x) for x in rooms)
        total += sum(padded_bytes(x) for n, x in enumerate(args) if n not in far)
        total += sum(padded_bytes(x) for n, x in enumerate(outs) if n not in far_out)
        specs = [SMEM if scalars[n] else FAR if n in far else FULL for n in range(len(args))]
        result = pl.pallas_call(
            kernel,
            out_shape=[pltpu.HBM(x.shape, x.dtype) if n in far_out else x for n, x in enumerate(outs)],
            in_specs=specs,
            out_specs=[FAR if n in far_out else FULL for n in range(len(outs))],
            scratch_shapes=[*rooms, pltpu.SemaphoreType.DMA((len(held) + len(written) + 1,))],
            compiler_params=pltpu.CompilerParams(vmem_limit_bytes=total + (3 << 20)),
        )(*[pltpu.with_memory_space_constraint(x, pltpu.HBM) if n in held else x for n, x in enumerate(args)])
        return result if isinstance(out, tuple) else result[0]

    return run


def shape(dims, dtype=BF16):
    return jax.ShapeDtypeStruct(dims, dtype)


def turn(parts):
    a = parts
    lane = lax.broadcasted_iota(jnp.int32, a[0].shape, 1)
    low = lane < 64
    even = (lane // 32) % 2 == 0

    def pair(x, y, mask, step):
        first = jnp.where(mask, x, pltpu.roll(y, step, 1))
        second = jnp.where(mask, pltpu.roll(x, 128 - step, 1), y)
        return first, second

    a0, a2 = pair(a[0], a[2], low, 64)
    a1, a3 = pair(a[1], a[3], low, 64)
    b0, b1 = pair(a0, a1, even, 32)
    b2, b3 = pair(a2, a3, even, 32)
    return [b0, b1, b2, b3]


def pack_kernel_body(core, taps, out):
    rows = []
    for t in range(HALF // 2):
        one = taps[core[0] * HALF + 2 * t].astype(F32)
        two = taps[core[0] * HALF + 2 * t + 1].astype(F32)
        rows.append(jnp.concatenate([one[:16], one[16:], two[:16], two[16:]], axis=1))
    block = jnp.concatenate(rows, axis=0).astype(BF16)
    out[...] = jnp.broadcast_to(block[None], out.shape)


def unpack_kernel_body(mine, out):
    def step(n, carry):
        for t in range(HALF // 2):
            for high in range(2):
                parts = [mine[8 * n + high * 4 + s, 16 * t : 16 * t + 16, :] for s in range(4)]
                for g, part in enumerate(turn(parts)):
                    rows = pl.ds(32 * n + 16 * (g % 2), 16)
                    out[2 * t + g // 2, rows, 128 * high : 128 * high + 128] = part
        return carry

    lax.fori_loop(0, 8, step, 0)


def pack_grad_body(kept, received, out):
    def step(n, carry):
        for t in range(HALF // 2):
            for high in range(2):
                parts = []
                for g in range(4):
                    slot, rows = 2 * t + g // 2, pl.ds(32 * n + 16 * (g % 2), 16)
                    lanes = pl.ds(128 * high, 128)
                    total = kept[slot, rows, lanes].astype(F32) + received[slot, rows, lanes].astype(F32)
                    parts.append(total.astype(BF16))
                for s, part in enumerate(turn(parts)):
                    out[8 * (high * 4 + s) + n, 16 * t : 16 * t + 16, :] = part
        return carry

    lax.fori_loop(0, 8, step, 0)


def sum_grad_body(blocks, out):
    total = blocks[0].astype(F32)
    for n in range(1, 64):
        total = total + blocks[n].astype(F32)
    out[...] = total


def unpack_grad_body(core, mine, other, out):
    zero = core[0] == 0
    first = jnp.where(zero, mine[...], other[...])
    second = jnp.where(zero, other[...], mine[...])
    for start, source in ((0, first), (13, second)):
        for t in range(HALF // 2):
            rows = source[16 * t : 16 * t + 16]
            for u in range(2):
                piece = jnp.concatenate([rows[:, 64 * u : 64 * u + 32], rows[:, 64 * u + 32 : 64 * u + 64]], axis=0)
                out[start + 2 * t + u] = piece.T


def blocks_of(place, turn_by, d):
    x, z = place[0] // 2, place[0] % 2
    column = (x + 4 + turn_by * d) % 4 * 2
    return column + z, column + 1 - z


def pack_cotangent_body(place, cot, keep, send):
    for d in range(4):
        for out, at in zip((keep, send), blocks_of(place, 1, d)):
            for s in range(2):
                parts = [cot[p, s, pl.ds(at * 4, 4)].reshape(128, 32).astype(F32) for p in range(4)]
                out[d, 128 * s : 128 * s + 128, :] = jnp.concatenate(parts, axis=1).astype(BF16)


def join_body(own, got, *outs):
    for d in range(4):
        outs[d][0] = own[d]
        outs[d][1] = got[d]


def unpack_output_body(place, *refs):
    out = refs[4]
    for d in range(4):
        for n, at in enumerate(blocks_of(place, -1, d)):
            for s in range(2):
                rows = refs[d][n, 128 * s : 128 * s + 128, :].astype(F32)
                for p in range(4):
                    out[p, s, pl.ds(at * 4, 4)] = rows[:, 32 * p : 32 * p + 32].reshape(4, 32, 32).astype(BF16)


def fill_shifts(pieces, target, window):
    middle, before, after = pieces[:3]
    window[0, :, 32:160, :] = before[0].reshape(2, 128, 256)
    window[1:5, :, 32:160, :] = middle[...].reshape(4, 2, 128, 256)
    window[5, :, 32:160, :] = after[0].reshape(2, 128, 256)
    for at, side in zip((0, 160), pieces[3:]):
        rows = jnp.zeros((6, 2, 32, 256), BF16) if side is None else side[...].reshape(6, 2, 32, 256)
        window[:, :, at : at + 32, :] = rows
    row = lax.broadcasted_iota(jnp.int32, (192, 256), 0) % 32

    def plane(n, carry):
        a, s = n // 2, n % 2
        x = window[a, s]
        wide = x.astype(F32)
        up = jnp.where(row == 0, 0.0, pltpu.roll(wide, 1, 0))
        down = jnp.where(row == 31, 0.0, pltpu.roll(wide, 191, 0))
        target[a, s, :, 0:256] = up.astype(BF16)
        target[a, s, :, 256:512] = x
        target[a, s, :, 512:768] = down.astype(BF16)
        return carry

    lax.fori_loop(0, 12, plane, 0)


def by_core(core, run, swap=0):
    @pl.when(core[0] == swap)
    def _():
        run(0)

    @pl.when(core[0] == 1 - swap)
    def _():
        run(1)


def edges_body(before, array, after, leading, last):
    for out, at in ((leading, 0), (last, 3)):
        out[0, :, 0] = before[0, :, at]
        out[1:5, :, 0] = array[:, :, at]
        out[5, :, 0] = after[0, :, at]


def groups_of(half):
    groups = []
    for tap in range(HALF * half, min(27, HALF * half + HALF)):
        i, j, k = tap // 9, tap // 3 % 3, tap % 3
        if groups and groups[-1][:2] == (i, j):
            groups[-1] = (i, j, groups[-1][2], groups[-1][3] + 1, groups[-1][4])
        else:
            groups.append((i, j, k, 1, tap - HALF * half))
    return groups


def conv_rows(shifts, weights, p, half):
    total = None
    for i, j, k, count, slot in groups_of(half):
        lanes = pl.ds(256 * k, 256 * count)
        lhs = shifts[p + i, :, 32 * j : 32 * j + 128, lanes].reshape(256, 256 * count)
        rhs = weights[slot : slot + count].reshape(256 * count, 256)
        term = jnp.dot(lhs, rhs, preferred_element_type=F32)
        total = term if total is None else total + term
    if half:
        total = total + weights[13, 0:1, :].astype(F32)
    return total


def forward_first_body(core, middle, before, after, left, right, mine, shifts, partial, window):
    fill_shifts((middle, before, after, left, right), shifts, window)

    def run(half):
        def plane(p, carry):
            partial[p] = conv_rows(shifts, mine, p, half)
            return carry

        lax.fori_loop(0, 4, plane, 0)

    by_core(core, run)


def forward_second_body(core, place, shifts, other, partial, *refs):
    grad_pre, keep, send, given, turned, blocks, cots, outs = refs[4:]
    for d, block in enumerate(refs[:4]):
        for n, at in enumerate(blocks_of(place, -1, d)):
            blocks[at] = block[n]
    for high in range(2):
        parts = turn([blocks[high * 4 + n] for n in range(4)])
        for p in range(4):
            cots[p, :, 128 * high : 128 * high + 128] = parts[p]

    def run(half):
        def plane(p, carry):
            hidden = partial[p] + conv_rows(shifts, other, p, half)
            gate = 1.0 / (1.0 + jnp.exp(-hidden))
            outs[p] = (hidden * gate).astype(BF16)
            slope = gate * (1.0 + hidden * (1.0 - gate))
            grad_pre[p] = (cots[p].astype(F32) * slope).astype(BF16).reshape(2, 4, 32, 256)
            return carry

        lax.fori_loop(0, 4, plane, 0)

    by_core(core, run, 1)
    for high in range(2):
        parts = turn([outs[p, :, 128 * high : 128 * high + 128] for p in range(4)])
        for n in range(4):
            blocks[high * 4 + n] = parts[n]
    for d in range(4):
        for out, at in zip((keep, send), blocks_of(place, 1, d)):
            out[d] = blocks[at]
    for p in range(4):
        turned[:, 256 * p : 256 * p + 256] = grad_pre[p].reshape(256, 256).astype(F32).T.astype(BF16)
    by_core(core, lambda half: tap_grads(shifts, turned, given, half), 1)


def tap_grads(shifts, turned, out, half):
    for i in range(3):
        for j in range(3):
            taps = [k for k in range(3) if 13 * half <= 9 * i + 3 * j + k < 13 * half + HALF]
            if taps:
                lanes = pl.ds(256 * taps[0], 256 * len(taps))
                rhs = shifts[i : i + 4, :, 32 * j : 32 * j + 128, lanes].reshape(1024, 256 * len(taps))
                res = jnp.dot(turned[...], rhs, preferred_element_type=F32).astype(BF16)
                for n, k in enumerate(taps):
                    out[9 * i + 3 * j + k - 13 * half] = res[:, 256 * n : 256 * n + 256]


def keep_grads_body(core, shifts, turned, received, out, kept):
    by_core(core, lambda half: tap_grads(shifts, turned, kept, half))
    pack_grad_body(kept, received, out)


def weight_of(mine, other, half, tap):
    first, second = (other, mine) if half else (mine, other)
    return first[tap] if tap < HALF else second[tap - HALF]


def back_dot(rows, weight):
    return lax.dot_general(rows, weight, (((1,), (1,)), ((), ())), preferred_element_type=F32)


def input_grad_body(core, middle, before, after, mine, other, inner, edges, shifts, window):
    fill_shifts((middle, before, after, None, None), shifts, window)

    def run(half):
        def plane(p, carry):
            total = jnp.zeros((256, 256), F32)
            for i in range(3):
                for j in range(3):
                    for k in range(3):
                        lanes = pl.ds(256 * (2 - k), 256)
                        lhs = shifts[p + 2 - i, :, 32 * (2 - j) : 32 * (2 - j) + 128, lanes].reshape(256, 256)
                        total = total + back_dot(lhs, weight_of(mine, other, half, 9 * i + 3 * j + k))
            rows = total.reshape(2, 4, 32, 256)
            inner[p] = rows[:, 1:3].astype(BF16)
            edges[p, :, 0] = rows[:, 0]
            edges[p, :, 1] = rows[:, 3]
            return carry

        lax.fori_loop(0, 4, plane, 0)

    by_core(core, run)


def edge_grad_body(core, left, right, mine, other, inner, edges, out, shifts):
    row = lax.broadcasted_iota(jnp.int32, (384, 256), 0) % 32
    for n, side in enumerate((left, right)):
        wide = side[...].reshape(384, 256).astype(F32)
        up = jnp.where(row == 0, 0.0, pltpu.roll(wide, 1, 0))
        down = jnp.where(row == 31, 0.0, pltpu.roll(wide, 383, 0))
        for k, part in enumerate((up, wide, down)):
            shifts[n, k] = part.astype(BF16).reshape(6, 64, 256)
    out[:, :, 1:3] = inner[...]

    def run(half):
        for n, (at, j) in enumerate(((0, 2), (3, 0))):
            total = edges[:, :, n].reshape(256, 256)
            for i in range(3):
                for k in range(3):
                    lhs = shifts[n, 2 - k, 2 - i : 6 - i].reshape(256, 256)
                    total = total + back_dot(lhs, weight_of(mine, other, half, 9 * i + 3 * j + k))
            out[:, :, at] = total.astype(BF16).reshape(4, 2, 32, 256)

    by_core(core, run)


SMEM = pl.BlockSpec(memory_space=pltpu.SMEM)
FULL = pl.BlockSpec(memory_space=pltpu.VMEM)
FAR = pl.BlockSpec(memory_space=pltpu.HBM)


def local(features, kernel, filter_bias, cotangent):
    core = lax.axis_index("sample").astype(jnp.int32)
    index = core[None]
    bias = jnp.broadcast_to(filter_bias[None, None, :], (1, 32, 32))
    taps = jnp.concatenate([kernel.reshape(27, 32, 32), bias], axis=0)
    place = lax.axis_index("sy").astype(jnp.int32)[None]
    four = shape((4, 256, 128))
    blocks = call(pack_kernel_body, shape((64, 112, 128)), far_out=(0,))(index, taps)
    keep, send = call(pack_cotangent_body, (four, four))(place, cotangent)
    before, after = halo(features, "sx", 0)
    got = swap_sides(send)
    blocks, before, after, keep, got = lax.optimization_barrier((blocks, before, after, keep, got))
    blocks = lax.all_to_all(blocks, GRID, 0, 0, tiled=True)
    left, right = corners(before, features, after)
    cot = spread(keep, got)
    mine = call(unpack_kernel_body, shape((HALF, 256, 256)), far=(0,))(blocks)
    mine, left, right, *cot = lax.optimization_barrier((mine, left, right, *cot))
    other = swap_cores(mine)
    shifts, partial = call(
        forward_first_body,
        (shape((6, 2, 192, 768)), shape((4, 256, 256), F32)),
        [pltpu.VMEM((6, 2, 192, 256), BF16)],
    )(index, features, before, after, left, right, mine)
    grad_pre, keep, send, given, turned = call(
        forward_second_body,
        (shape((4, 2, 4, 32, 256)), four, four, shape((HALF, 256, 256)), shape((256, 1024))),
        [pltpu.VMEM((8, 256, 128), BF16), pltpu.VMEM((4, 256, 256), BF16), pltpu.VMEM((4, 256, 256), BF16)],
    )(index, place, shifts, other, partial, *cot)
    before, after = halo(grad_pre, "sx", 0)
    got = swap_sides(send)
    received = swap_cores(given)
    turned, before, after, got = lax.optimization_barrier((turned, before, after, got))
    blocks = call(
        keep_grads_body, shape((64, 112, 128)), [pltpu.VMEM((HALF, 256, 256), BF16)], far_out=(0,)
    )(index, shifts, turned, received)
    blocks, before, after, keep, got = lax.optimization_barrier((blocks, before, after, keep, got))
    left, right = corners(before, grad_pre, after)
    blocks = lax.all_to_all(blocks, GRID, 0, 0, tiled=True)
    pieces = spread(keep, got)
    half = shape((4, 2, 2, 32, 256))
    inner, edges = call(
        input_grad_body,
        (half, shape((4, 2, 2, 32, 256), F32)),
        [pltpu.VMEM((6, 2, 192, 768), BF16), pltpu.VMEM((6, 2, 192, 256), BF16)],
        far=(1, 2, 3, 4, 5),
        far_out=(0, 1),
    )(index, grad_pre, before, after, mine, other)
    blocks, inner, edges = lax.optimization_barrier((blocks, inner, edges))
    rows = call(sum_grad_body, shape((112, 128), F32))(blocks)
    rows, left, right = lax.optimization_barrier((rows, left, right))
    turned_rows = swap_cores(rows)
    input_grad = call(
        edge_grad_body,
        shape((4, 2, 4, 32, 256)),
        [pltpu.VMEM((2, 3, 6, 64, 256), BF16)],
        far=(3, 4, 5, 6),
    )(index, left, right, mine, other, inner, edges)
    input_grad, *pieces = lax.optimization_barrier((input_grad, *pieces))
    output = call(unpack_output_body, shape((4, 2, 32, 32, 32)))(place, *pieces)
    kernel_grad = call(unpack_grad_body, shape((27, 32, 32), F32))(index, rows, turned_rows)
    return (output, input_grad, kernel_grad.reshape(3, 3, 3, 32, 32))


def solution(mesh):
    return jax.shard_map(
        local,
        mesh=mesh,
        in_specs=(
            P("sx", "sample", "sy", None, None),
            P(None, None, None, "sx", "sy"),
            P("sy"),
            P("sx", "sample", None, None, "sy"),
        ),
        out_specs=(
            P("sx", "sample", None, None, "sy"),
            P("sx", "sample", "sy", None, None),
            P(None, None, None, "sx", "sy"),
        ),
        check_vma=False,
    )
```

```python
import jax
import jax.numpy as jnp
from jax import lax
from jax.experimental import pallas as pl
from jax.experimental.pallas import tpu as pltpu
from jax.sharding import PartitionSpec as P

HALF = 14
GRID = ("sx", "sy")
BF16 = jnp.bfloat16
F32 = jnp.float32


def halo(array, axis, dim):
    size, length = (lax.axis_size(axis), array.shape[dim])
    up = [(i, i + 1) for i in range(size - 1)]
    down = [(j, i) for i, j in up]
    last = lax.slice_in_dim(array, length - 1, length, axis=dim)
    leading = lax.slice_in_dim(array, 0, 1, axis=dim)
    return lax.ppermute(last, axis, up), lax.ppermute(leading, axis, down)


def corners(before, array, after):
    edge = shape((6, 2, 1, 32, 256))
    leading, last = call(edges_body, (edge, edge))(before, array, after)
    up = [(i, i + 1) for i in range(7)]
    down = [(j, i) for i, j in up]
    return lax.ppermute(last, "sy", up), lax.ppermute(leading, "sy", down)


def swap_cores(array):
    return lax.ppermute(array, "sample", [(0, 1), (1, 0)])


def swap_sides(array):
    return lax.ppermute(array, "sy", [(i, i + 1 - 2 * (i % 2)) for i in range(8)])


def spread(own, got):
    pieces = call(join_body, tuple(shape((2, 256, 128)) for _ in range(4)))(own, got)
    moved = [
        lax.ppermute(pieces[d], "sy", [(i, (i // 2 + d) % 4 * 2 + i % 2) for i in range(8)]) for d in range(1, 4)
    ]
    return [pieces[0], *moved]


def padded_bytes(x):
    dims = [1, *x.shape]
    lanes, rows = -(-dims[-1] // 128) * 128, -(-dims[-2] // 16) * 16
    size = lanes * rows * jnp.dtype(x.dtype).itemsize
    for dim in dims[:-2]:
        size *= dim
    return size


def call(body, out, scratch=(), far=(), far_out=(), parts=0):
    outs = list(out) if isinstance(out, tuple) else [out]

    def run(*args):
        scalars = [x.dtype == jnp.int32 for x in args]
        held = list(far)
        written = list(far_out)

        def kernel(*refs):
            count = len(args) + len(outs)
            near = list(refs[:count])
            extra = refs[count:]
            sems = extra[-1]
            pieces = max(parts, 1)

            def copy_in(at, piece):
                size = args[held[at]].shape[0] // pieces
                rows = pl.ds(piece * size, size)
                return pltpu.make_async_copy(
                    refs[held[at]].at[rows], extra[at].at[rows], sems.at[at * pieces + piece]
                )

            def wait(piece):
                for at in range(len(held)):
                    copy_in(at, piece).wait()

            for at, n in enumerate(held):
                near[n] = extra[at]
            for piece in range(pieces):
                for at in range(len(held)):
                    copy_in(at, piece).start()
            for at, n in enumerate(written):
                near[len(args) + n] = extra[len(held) + at]
            if not parts:
                wait(0)
            given = (wait,) if parts else ()
            body(*near, *extra[len(held) + len(written) : -1], *given)
            copies = []
            for at, n in enumerate(written):
                to = refs[len(args) + n]
                copies.append(pltpu.make_async_copy(near[len(args) + n], to, sems.at[len(held) * pieces + at]))
            for copy in copies:
                copy.start()
            for copy in copies:
                copy.wait()

        rooms = [pltpu.VMEM(args[n].shape, args[n].dtype) for n in held]
        rooms += [pltpu.VMEM(outs[n].shape, outs[n].dtype) for n in written]
        rooms += list(scratch)
        total = sum(padded_bytes(x) for x in rooms)
        total += sum(padded_bytes(x) for n, x in enumerate(args) if n not in far)
        total += sum(padded_bytes(x) for n, x in enumerate(outs) if n not in far_out)
        specs = [SMEM if scalars[n] else FAR if n in far else FULL for n in range(len(args))]
        result = pl.pallas_call(
            kernel,
            out_shape=[pltpu.HBM(x.shape, x.dtype) if n in far_out else x for n, x in enumerate(outs)],
            in_specs=specs,
            out_specs=[FAR if n in far_out else FULL for n in range(len(outs))],
            scratch_shapes=[*rooms, pltpu.SemaphoreType.DMA((len(held) * max(parts, 1) + len(written) + 1,))],
            compiler_params=pltpu.CompilerParams(vmem_limit_bytes=total + (3 << 20)),
        )(*[pltpu.with_memory_space_constraint(x, pltpu.HBM) if n in held else x for n, x in enumerate(args)])
        return result if isinstance(out, tuple) else result[0]

    return run


def shape(dims, dtype=BF16):
    return jax.ShapeDtypeStruct(dims, dtype)


def turn(parts):
    a = parts
    lane = lax.broadcasted_iota(jnp.int32, a[0].shape, 1)
    low = lane < 64
    even = (lane // 32) % 2 == 0

    def pair(x, y, mask, step):
        first = jnp.where(mask, x, pltpu.roll(y, step, 1))
        second = jnp.where(mask, pltpu.roll(x, 128 - step, 1), y)
        return first, second

    a0, a2 = pair(a[0], a[2], low, 64)
    a1, a3 = pair(a[1], a[3], low, 64)
    b0, b1 = pair(a0, a1, even, 32)
    b2, b3 = pair(a2, a3, even, 32)
    return [b0, b1, b2, b3]


def pack_kernel_body(core, taps, out):
    rows = []
    for t in range(HALF // 2):
        one = taps[core[0] * HALF + 2 * t].astype(F32)
        two = taps[core[0] * HALF + 2 * t + 1].astype(F32)
        rows.append(jnp.concatenate([one[:16], one[16:], two[:16], two[16:]], axis=1))
    block = jnp.concatenate(rows, axis=0).astype(BF16)
    out[...] = jnp.broadcast_to(block[None], out.shape)


def unpack_kernel_body(mine, out, wait):
    def step(n, carry):
        wait(n)
        for t in range(HALF // 2):
            for high in range(2):
                parts = [mine[8 * n + high * 4 + s, 16 * t : 16 * t + 16, :] for s in range(4)]
                for g, part in enumerate(turn(parts)):
                    rows = pl.ds(32 * n + 16 * (g % 2), 16)
                    out[2 * t + g // 2, rows, 128 * high : 128 * high + 128] = part
        return carry

    lax.fori_loop(0, 8, step, 0)


def pack_grad_body(kept, received, out):
    def step(n, carry):
        for t in range(HALF // 2):
            for high in range(2):
                parts = []
                for g in range(4):
                    slot, rows = 2 * t + g // 2, pl.ds(32 * n + 16 * (g % 2), 16)
                    lanes = pl.ds(128 * high, 128)
                    total = kept[slot, rows, lanes].astype(F32) + received[slot, rows, lanes].astype(F32)
                    parts.append(total.astype(BF16))
                for s, part in enumerate(turn(parts)):
                    out[8 * (high * 4 + s) + n, 16 * t : 16 * t + 16, :] = part
        return carry

    lax.fori_loop(0, 8, step, 0)


def sum_grad_body(blocks, out):
    total = blocks[0].astype(F32)
    for n in range(1, 64):
        total = total + blocks[n].astype(F32)
    out[...] = total


def unpack_grad_body(core, mine, other, out):
    zero = core[0] == 0
    first = jnp.where(zero, mine[...], other[...])
    second = jnp.where(zero, other[...], mine[...])
    for start, source in ((0, first), (13, second)):
        for t in range(HALF // 2):
            rows = source[16 * t : 16 * t + 16]
            for u in range(2):
                piece = jnp.concatenate([rows[:, 64 * u : 64 * u + 32], rows[:, 64 * u + 32 : 64 * u + 64]], axis=0)
                out[start + 2 * t + u] = piece.T


def blocks_of(place, turn_by, d):
    x, z = place[0] // 2, place[0] % 2
    column = (x + 4 + turn_by * d) % 4 * 2
    return column + z, column + 1 - z


def pack_cotangent_body(place, cot, keep, send):
    for d in range(4):
        for out, at in zip((keep, send), blocks_of(place, 1, d)):
            for s in range(2):
                parts = [cot[p, s, pl.ds(at * 4, 4)].reshape(128, 32).astype(F32) for p in range(4)]
                out[d, 128 * s : 128 * s + 128, :] = jnp.concatenate(parts, axis=1).astype(BF16)


def join_body(own, got, *outs):
    for d in range(4):
        outs[d][0] = own[d]
        outs[d][1] = got[d]


def unpack_output_body(place, *refs):
    out = refs[4]
    for d in range(4):
        for n, at in enumerate(blocks_of(place, -1, d)):
            for s in range(2):
                rows = refs[d][n, 128 * s : 128 * s + 128, :].astype(F32)
                for p in range(4):
                    out[p, s, pl.ds(at * 4, 4)] = rows[:, 32 * p : 32 * p + 32].reshape(4, 32, 32).astype(BF16)


def fill_shifts(pieces, target, window):
    middle, before, after = pieces[:3]
    window[0, :, 32:160, :] = before[0].reshape(2, 128, 256)
    window[1:5, :, 32:160, :] = middle[...].reshape(4, 2, 128, 256)
    window[5, :, 32:160, :] = after[0].reshape(2, 128, 256)
    for at, side in zip((0, 160), pieces[3:]):
        rows = jnp.zeros((6, 2, 32, 256), BF16) if side is None else side[...].reshape(6, 2, 32, 256)
        window[:, :, at : at + 32, :] = rows
    row = lax.broadcasted_iota(jnp.int32, (192, 256), 0) % 32

    def plane(n, carry):
        a, s = n // 2, n % 2
        x = window[a, s]
        wide = x.astype(F32)
        up = jnp.where(row == 0, 0.0, pltpu.roll(wide, 1, 0))
        down = jnp.where(row == 31, 0.0, pltpu.roll(wide, 191, 0))
        target[a, s, :, 0:256] = up.astype(BF16)
        target[a, s, :, 256:512] = x
        target[a, s, :, 512:768] = down.astype(BF16)
        return carry

    lax.fori_loop(0, 12, plane, 0)


def by_core(core, run, swap=0):
    @pl.when(core[0] == swap)
    def _():
        run(0)

    @pl.when(core[0] == 1 - swap)
    def _():
        run(1)


def edges_body(before, array, after, leading, last):
    for out, at in ((leading, 0), (last, 3)):
        out[0, :, 0] = before[0, :, at]
        out[1:5, :, 0] = array[:, :, at]
        out[5, :, 0] = after[0, :, at]


def groups_of(half):
    groups = []
    for tap in range(HALF * half, min(27, HALF * half + HALF)):
        i, j, k = tap // 9, tap // 3 % 3, tap % 3
        if groups and groups[-1][:2] == (i, j):
            groups[-1] = (i, j, groups[-1][2], groups[-1][3] + 1, groups[-1][4])
        else:
            groups.append((i, j, k, 1, tap - HALF * half))
    return groups


def conv_rows(shifts, weights, p, half):
    total = None
    for i, j, k, count, slot in groups_of(half):
        lanes = pl.ds(256 * k, 256 * count)
        lhs = shifts[p + i, :, 32 * j : 32 * j + 128, lanes].reshape(256, 256 * count)
        rhs = weights[slot : slot + count].reshape(256 * count, 256)
        term = jnp.dot(lhs, rhs, preferred_element_type=F32)
        total = term if total is None else total + term
    if half:
        total = total + weights[13, 0:1, :].astype(F32)
    return total


def forward_first_body(core, middle, before, after, left, right, mine, shifts, partial, window):
    fill_shifts((middle, before, after, left, right), shifts, window)

    def run(half):
        def plane(p, carry):
            partial[p] = conv_rows(shifts, mine, p, half)
            return carry

        lax.fori_loop(0, 4, plane, 0)

    by_core(core, run)


def forward_second_body(core, place, shifts, other, partial, *refs):
    grad_pre, keep, send, given, turned, blocks, cots, outs = refs[4:]
    for d, block in enumerate(refs[:4]):
        for n, at in enumerate(blocks_of(place, -1, d)):
            blocks[at] = block[n]
    for high in range(2):
        parts = turn([blocks[high * 4 + n] for n in range(4)])
        for p in range(4):
            cots[p, :, 128 * high : 128 * high + 128] = parts[p]

    def run(half):
        def plane(p, carry):
            hidden = partial[p] + conv_rows(shifts, other, p, half)
            gate = 1.0 / (1.0 + jnp.exp(-hidden))
            outs[p] = (hidden * gate).astype(BF16)
            slope = gate * (1.0 + hidden * (1.0 - gate))
            grad_pre[p] = (cots[p].astype(F32) * slope).astype(BF16).reshape(2, 4, 32, 256)
            return carry

        lax.fori_loop(0, 4, plane, 0)

    by_core(core, run, 1)
    for high in range(2):
        parts = turn([outs[p, :, 128 * high : 128 * high + 128] for p in range(4)])
        for n in range(4):
            blocks[high * 4 + n] = parts[n]
    for d in range(4):
        for out, at in zip((keep, send), blocks_of(place, 1, d)):
            out[d] = blocks[at]
    for p in range(4):
        turned[:, 256 * p : 256 * p + 256] = grad_pre[p].reshape(256, 256).astype(F32).T.astype(BF16)
    by_core(core, lambda half: tap_grads(shifts, turned, given, half), 1)


def tap_grads(shifts, turned, out, half):
    for i in range(3):
        for j in range(3):
            taps = [k for k in range(3) if 13 * half <= 9 * i + 3 * j + k < 13 * half + HALF]
            if taps:
                lanes = pl.ds(256 * taps[0], 256 * len(taps))
                rhs = shifts[i : i + 4, :, 32 * j : 32 * j + 128, lanes].reshape(1024, 256 * len(taps))
                res = jnp.dot(turned[...], rhs, preferred_element_type=F32).astype(BF16)
                for n, k in enumerate(taps):
                    out[9 * i + 3 * j + k - 13 * half] = res[:, 256 * n : 256 * n + 256]


def keep_grads_body(core, shifts, turned, received, out, kept):
    by_core(core, lambda half: tap_grads(shifts, turned, kept, half))
    pack_grad_body(kept, received, out)


def weight_of(mine, other, half, tap):
    first, second = (other, mine) if half else (mine, other)
    return first[tap] if tap < HALF else second[tap - HALF]


def back_dot(rows, weight):
    return lax.dot_general(rows, weight, (((1,), (1,)), ((), ())), preferred_element_type=F32)


def input_grad_body(core, middle, before, after, mine, other, inner, edges, shifts, window):
    fill_shifts((middle, before, after, None, None), shifts, window)

    def run(half):
        def plane(p, carry):
            total = jnp.zeros((256, 256), F32)
            for i in range(3):
                for j in range(3):
                    for k in range(3):
                        lanes = pl.ds(256 * (2 - k), 256)
                        lhs = shifts[p + 2 - i, :, 32 * (2 - j) : 32 * (2 - j) + 128, lanes].reshape(256, 256)
                        total = total + back_dot(lhs, weight_of(mine, other, half, 9 * i + 3 * j + k))
            rows = total.reshape(2, 4, 32, 256)
            inner[p] = rows[:, 1:3].astype(BF16)
            edges[p, :, 0] = rows[:, 0]
            edges[p, :, 1] = rows[:, 3]
            return carry

        lax.fori_loop(0, 4, plane, 0)

    by_core(core, run)


def edge_grad_body(core, left, right, mine, other, inner, edges, out, shifts, wait):
    row = lax.broadcasted_iota(jnp.int32, (384, 256), 0) % 32
    for n, side in enumerate((left, right)):
        wide = side[...].reshape(384, 256).astype(F32)
        up = jnp.where(row == 0, 0.0, pltpu.roll(wide, 1, 0))
        down = jnp.where(row == 31, 0.0, pltpu.roll(wide, 383, 0))
        for k, part in enumerate((up, wide, down)):
            shifts[n, k] = part.astype(BF16).reshape(6, 64, 256)
    wait(0)
    out[:, :, 1:3] = inner[...]

    def run(half):
        for n, (at, j) in enumerate(((0, 2), (3, 0))):
            total = edges[:, :, n].reshape(256, 256)
            for i in range(3):
                for k in range(3):
                    lhs = shifts[n, 2 - k, 2 - i : 6 - i].reshape(256, 256)
                    total = total + back_dot(lhs, weight_of(mine, other, half, 9 * i + 3 * j + k))
            out[:, :, at] = total.astype(BF16).reshape(4, 2, 32, 256)

    by_core(core, run)


SMEM = pl.BlockSpec(memory_space=pltpu.SMEM)
FULL = pl.BlockSpec(memory_space=pltpu.VMEM)
FAR = pl.BlockSpec(memory_space=pltpu.HBM)


def local(features, kernel, filter_bias, cotangent):
    core = lax.axis_index("sample").astype(jnp.int32)
    index = core[None]
    bias = jnp.broadcast_to(filter_bias[None, None, :], (1, 32, 32))
    taps = jnp.concatenate([kernel.reshape(27, 32, 32), bias], axis=0)
    place = lax.axis_index("sy").astype(jnp.int32)[None]
    four = shape((4, 256, 128))
    blocks = call(pack_kernel_body, shape((64, 112, 128)), far_out=(0,))(index, taps)
    keep, send = call(pack_cotangent_body, (four, four))(place, cotangent)
    before, after = halo(features, "sx", 0)
    got = swap_sides(send)
    blocks, before, after, keep, got = lax.optimization_barrier((blocks, before, after, keep, got))
    blocks = lax.all_to_all(blocks, GRID, 0, 0, tiled=True)
    left, right = corners(before, features, after)
    cot = spread(keep, got)
    mine = call(unpack_kernel_body, shape((HALF, 256, 256)), far=(0,), parts=8)(blocks)
    mine, left, right, *cot = lax.optimization_barrier((mine, left, right, *cot))
    other = swap_cores(mine)
    shifts, partial = call(
        forward_first_body,
        (shape((6, 2, 192, 768)), shape((4, 256, 256), F32)),
        [pltpu.VMEM((6, 2, 192, 256), BF16)],
    )(index, features, before, after, left, right, mine)
    grad_pre, keep, send, given, turned = call(
        forward_second_body,
        (shape((4, 2, 4, 32, 256)), four, four, shape((HALF, 256, 256)), shape((256, 1024))),
        [pltpu.VMEM((8, 256, 128), BF16), pltpu.VMEM((4, 256, 256), BF16), pltpu.VMEM((4, 256, 256), BF16)],
    )(index, place, shifts, other, partial, *cot)
    before, after = halo(grad_pre, "sx", 0)
    got = swap_sides(send)
    received = swap_cores(given)
    blocks = call(
        keep_grads_body, shape((64, 112, 128)), [pltpu.VMEM((HALF, 256, 256), BF16)], far_out=(0,)
    )(index, shifts, turned, received)
    blocks, before, after, keep, got = lax.optimization_barrier((blocks, before, after, keep, got))
    left, right = corners(before, grad_pre, after)
    blocks = lax.all_to_all(blocks, GRID, 0, 0, tiled=True)
    pieces = spread(keep, got)
    half = shape((4, 2, 2, 32, 256))
    inner, edges = call(
        input_grad_body,
        (half, shape((4, 2, 2, 32, 256), F32)),
        [pltpu.VMEM((6, 2, 192, 768), BF16), pltpu.VMEM((6, 2, 192, 256), BF16)],
        far=(1, 2, 3, 4, 5),
        far_out=(0, 1),
    )(index, grad_pre, before, after, mine, other)
    blocks, inner, edges = lax.optimization_barrier((blocks, inner, edges))
    rows = call(sum_grad_body, shape((112, 128), F32))(blocks)
    rows, left, right = lax.optimization_barrier((rows, left, right))
    turned_rows = swap_cores(rows)
    input_grad = call(
        edge_grad_body,
        shape((4, 2, 4, 32, 256)),
        [pltpu.VMEM((2, 3, 6, 64, 256), BF16)],
        far=(3, 4, 5, 6),
        parts=1,
    )(index, left, right, mine, other, inner, edges)
    input_grad, *pieces = lax.optimization_barrier((input_grad, *pieces))
    output = call(unpack_output_body, shape((4, 2, 32, 32, 32)))(place, *pieces)
    kernel_grad = call(unpack_grad_body, shape((27, 32, 32), F32))(index, rows, turned_rows)
    return (output, input_grad, kernel_grad.reshape(3, 3, 3, 32, 32))


def solution(mesh):
    return jax.shard_map(
        local,
        mesh=mesh,
        in_specs=(
            P("sx", "sample", "sy", None, None),
            P(None, None, None, "sx", "sy"),
            P("sy"),
            P("sx", "sample", None, None, "sy"),
        ),
        out_specs=(
            P("sx", "sample", None, None, "sy"),
            P("sx", "sample", "sy", None, None),
            P(None, None, None, "sx", "sy"),
        ),
        check_vma=False,
    )
```

```python
import jax
import jax.numpy as jnp
from jax import lax
from jax.experimental import pallas as pl
from jax.experimental.pallas import tpu as pltpu
from jax.sharding import PartitionSpec as P

HALF = 14
GRID = ("sx", "sy")
BF16 = jnp.bfloat16
F32 = jnp.float32


def halo(array, axis, dim):
    size, length = (lax.axis_size(axis), array.shape[dim])
    up = [(i, i + 1) for i in range(size - 1)]
    down = [(j, i) for i, j in up]
    last = lax.slice_in_dim(array, length - 1, length, axis=dim)
    leading = lax.slice_in_dim(array, 0, 1, axis=dim)
    return lax.ppermute(last, axis, up), lax.ppermute(leading, axis, down)


def corners(before, array, after):
    edge = shape((6, 2, 1, 32, 256))
    leading, last = call(edges_body, (edge, edge))(before, array, after)
    up = [(i, i + 1) for i in range(7)]
    down = [(j, i) for i, j in up]
    return lax.ppermute(last, "sy", up), lax.ppermute(leading, "sy", down)


def swap_cores(array):
    return lax.ppermute(array, "sample", [(0, 1), (1, 0)])


def swap_sides(array):
    return lax.ppermute(array, "sy", [(i, i + 1 - 2 * (i % 2)) for i in range(8)])


def spread(own, got):
    pieces = call(join_body, tuple(shape((2, 256, 128)) for _ in range(4)))(own, got)
    moved = [
        lax.ppermute(pieces[d], "sy", [(i, (i // 2 + d) % 4 * 2 + i % 2) for i in range(8)]) for d in range(1, 4)
    ]
    return [pieces[0], *moved]


def padded_bytes(x):
    dims = [1, *x.shape]
    lanes, rows = -(-dims[-1] // 128) * 128, -(-dims[-2] // 16) * 16
    size = lanes * rows * jnp.dtype(x.dtype).itemsize
    for dim in dims[:-2]:
        size *= dim
    return size


def call(body, out, scratch=(), far=(), far_out=(), parts=0, parts_out=0):
    outs = list(out) if isinstance(out, tuple) else [out]

    def run(*args):
        scalars = [x.dtype == jnp.int32 for x in args]
        held = list(far)
        written = list(far_out)

        def kernel(*refs):
            count = len(args) + len(outs)
            near = list(refs[:count])
            extra = refs[count:]
            sems = extra[-1]
            pieces = max(parts, 1)

            def copy_in(at, piece):
                size = args[held[at]].shape[0] // pieces
                rows = pl.ds(piece * size, size)
                return pltpu.make_async_copy(
                    refs[held[at]].at[rows], extra[at].at[rows], sems.at[at * pieces + piece]
                )

            def wait(piece):
                for at in range(len(held)):
                    copy_in(at, piece).wait()

            for at, n in enumerate(held):
                near[n] = extra[at]
            for piece in range(pieces):
                for at in range(len(held)):
                    copy_in(at, piece).start()
            for at, n in enumerate(written):
                near[len(args) + n] = extra[len(held) + at]
            if not parts:
                wait(0)
            out_pieces = max(parts_out, 1)

            def copy_out(at, piece):
                n = written[at]
                size = outs[n].shape[0] // out_pieces
                rows = pl.ds(piece * size, size)
                sem = sems.at[len(held) * pieces + at * out_pieces + piece]
                return pltpu.make_async_copy(near[len(args) + n].at[rows], refs[len(args) + n].at[rows], sem)

            def send(piece):
                for at in range(len(written)):
                    copy_out(at, piece).start()

            given = ((wait,) if parts else ()) + ((send,) if parts_out else ())
            body(*near, *extra[len(held) + len(written) : -1], *given)
            if not parts_out:
                send(0)
            for piece in range(out_pieces):
                for at in range(len(written)):
                    copy_out(at, piece).wait()

        rooms = [pltpu.VMEM(args[n].shape, args[n].dtype) for n in held]
        rooms += [pltpu.VMEM(outs[n].shape, outs[n].dtype) for n in written]
        rooms += list(scratch)
        total = sum(padded_bytes(x) for x in rooms)
        total += sum(padded_bytes(x) for n, x in enumerate(args) if n not in far)
        total += sum(padded_bytes(x) for n, x in enumerate(outs) if n not in far_out)
        specs = [SMEM if scalars[n] else FAR if n in far else FULL for n in range(len(args))]
        result = pl.pallas_call(
            kernel,
            out_shape=[pltpu.HBM(x.shape, x.dtype) if n in far_out else x for n, x in enumerate(outs)],
            in_specs=specs,
            out_specs=[FAR if n in far_out else FULL for n in range(len(outs))],
            scratch_shapes=[*rooms, pltpu.SemaphoreType.DMA((len(held) * max(parts, 1) + len(written) * max(parts_out, 1) + 1,))],
            compiler_params=pltpu.CompilerParams(vmem_limit_bytes=total + (3 << 20)),
        )(*[pltpu.with_memory_space_constraint(x, pltpu.HBM) if n in held else x for n, x in enumerate(args)])
        return result if isinstance(out, tuple) else result[0]

    return run


def shape(dims, dtype=BF16):
    return jax.ShapeDtypeStruct(dims, dtype)


def turn(parts):
    a = parts
    lane = lax.broadcasted_iota(jnp.int32, a[0].shape, 1)
    low = lane < 64
    even = (lane // 32) % 2 == 0

    def pair(x, y, mask, step):
        first = jnp.where(mask, x, pltpu.roll(y, step, 1))
        second = jnp.where(mask, pltpu.roll(x, 128 - step, 1), y)
        return first, second

    a0, a2 = pair(a[0], a[2], low, 64)
    a1, a3 = pair(a[1], a[3], low, 64)
    b0, b1 = pair(a0, a1, even, 32)
    b2, b3 = pair(a2, a3, even, 32)
    return [b0, b1, b2, b3]


def pack_kernel_body(core, taps, out):
    rows = []
    for t in range(HALF // 2):
        one = taps[core[0] * HALF + 2 * t].astype(F32)
        two = taps[core[0] * HALF + 2 * t + 1].astype(F32)
        rows.append(jnp.concatenate([one[:16], one[16:], two[:16], two[16:]], axis=1))
    block = jnp.concatenate(rows, axis=0).astype(BF16)
    out[...] = jnp.broadcast_to(block[None], out.shape)


def unpack_kernel_body(mine, out, wait):
    def step(n, carry):
        wait(n)
        for t in range(HALF // 2):
            for high in range(2):
                parts = [mine[8 * n + high * 4 + s, 16 * t : 16 * t + 16, :] for s in range(4)]
                for g, part in enumerate(turn(parts)):
                    rows = pl.ds(32 * n + 16 * (g % 2), 16)
                    out[2 * t + g // 2, rows, 128 * high : 128 * high + 128] = part
        return carry

    lax.fori_loop(0, 8, step, 0)


def pack_grad_body(kept, received, out):
    def step(n, carry):
        for t in range(HALF // 2):
            for high in range(2):
                parts = []
                for g in range(4):
                    slot, rows = 2 * t + g // 2, pl.ds(32 * n + 16 * (g % 2), 16)
                    lanes = pl.ds(128 * high, 128)
                    total = kept[slot, rows, lanes].astype(F32) + received[slot, rows, lanes].astype(F32)
                    parts.append(total.astype(BF16))
                for s, part in enumerate(turn(parts)):
                    out[8 * (high * 4 + s) + n, 16 * t : 16 * t + 16, :] = part
        return carry

    lax.fori_loop(0, 8, step, 0)


def sum_grad_body(blocks, out):
    total = blocks[0].astype(F32)
    for n in range(1, 64):
        total = total + blocks[n].astype(F32)
    out[...] = total


def unpack_grad_body(core, mine, other, out):
    zero = core[0] == 0
    first = jnp.where(zero, mine[...], other[...])
    second = jnp.where(zero, other[...], mine[...])
    for start, source in ((0, first), (13, second)):
        for t in range(HALF // 2):
            rows = source[16 * t : 16 * t + 16]
            for u in range(2):
                piece = jnp.concatenate([rows[:, 64 * u : 64 * u + 32], rows[:, 64 * u + 32 : 64 * u + 64]], axis=0)
                out[start + 2 * t + u] = piece.T


def blocks_of(place, turn_by, d):
    x, z = place[0] // 2, place[0] % 2
    column = (x + 4 + turn_by * d) % 4 * 2
    return column + z, column + 1 - z


def pack_cotangent_body(place, cot, keep, send):
    for d in range(4):
        for out, at in zip((keep, send), blocks_of(place, 1, d)):
            for s in range(2):
                parts = [cot[p, s, pl.ds(at * 4, 4)].reshape(128, 32).astype(F32) for p in range(4)]
                out[d, 128 * s : 128 * s + 128, :] = jnp.concatenate(parts, axis=1).astype(BF16)


def join_body(own, got, *outs):
    for d in range(4):
        outs[d][0] = own[d]
        outs[d][1] = got[d]


def finish_body(core, place, mine, other, *refs):
    out, grad, send = refs[4:]
    for p in range(4):
        for d in range(4):
            for n, at in enumerate(blocks_of(place, -1, d)):
                for s in range(2):
                    rows = refs[d][n, 128 * s : 128 * s + 128, :].astype(F32)
                    out[p, s, pl.ds(at * 4, 4)] = rows[:, 32 * p : 32 * p + 32].reshape(4, 32, 32).astype(BF16)
        send(p)
    unpack_grad_body(core, mine, other, grad)


def fill_shifts(pieces, target, window):
    middle, before, after = pieces[:3]
    window[0, :, 32:160, :] = before[0].reshape(2, 128, 256)
    window[1:5, :, 32:160, :] = middle[...].reshape(4, 2, 128, 256)
    window[5, :, 32:160, :] = after[0].reshape(2, 128, 256)
    for at, side in zip((0, 160), pieces[3:]):
        rows = jnp.zeros((6, 2, 32, 256), BF16) if side is None else side[...].reshape(6, 2, 32, 256)
        window[:, :, at : at + 32, :] = rows
    row = lax.broadcasted_iota(jnp.int32, (192, 256), 0) % 32

    def plane(n, carry):
        a, s = n // 2, n % 2
        x = window[a, s]
        wide = x.astype(F32)
        up = jnp.where(row == 0, 0.0, pltpu.roll(wide, 1, 0))
        down = jnp.where(row == 31, 0.0, pltpu.roll(wide, 191, 0))
        target[a, s, :, 0:256] = up.astype(BF16)
        target[a, s, :, 256:512] = x
        target[a, s, :, 512:768] = down.astype(BF16)
        return carry

    lax.fori_loop(0, 12, plane, 0)


def by_core(core, run, swap=0):
    @pl.when(core[0] == swap)
    def _():
        run(0)

    @pl.when(core[0] == 1 - swap)
    def _():
        run(1)


def edges_body(before, array, after, leading, last):
    for out, at in ((leading, 0), (last, 3)):
        out[0, :, 0] = before[0, :, at]
        out[1:5, :, 0] = array[:, :, at]
        out[5, :, 0] = after[0, :, at]


def groups_of(half):
    groups = []
    for tap in range(HALF * half, min(27, HALF * half + HALF)):
        i, j, k = tap // 9, tap // 3 % 3, tap % 3
        if groups and groups[-1][:2] == (i, j):
            groups[-1] = (i, j, groups[-1][2], groups[-1][3] + 1, groups[-1][4])
        else:
            groups.append((i, j, k, 1, tap - HALF * half))
    return groups


def conv_rows(shifts, weights, p, half):
    total = None
    for i, j, k, count, slot in groups_of(half):
        lanes = pl.ds(256 * k, 256 * count)
        lhs = shifts[p + i, :, 32 * j : 32 * j + 128, lanes].reshape(256, 256 * count)
        rhs = weights[slot : slot + count].reshape(256 * count, 256)
        term = jnp.dot(lhs, rhs, preferred_element_type=F32)
        total = term if total is None else total + term
    if half:
        total = total + weights[13, 0:1, :].astype(F32)
    return total


def forward_first_body(core, middle, before, after, left, right, mine, shifts, partial, window):
    fill_shifts((middle, before, after, left, right), shifts, window)

    def run(half):
        def plane(p, carry):
            partial[p] = conv_rows(shifts, mine, p, half)
            return carry

        lax.fori_loop(0, 4, plane, 0)

    by_core(core, run)


def forward_second_body(core, place, shifts, other, partial, *refs):
    grad_pre, keep, send, given, turned, blocks, cots, outs = refs[4:]
    for d, block in enumerate(refs[:4]):
        for n, at in enumerate(blocks_of(place, -1, d)):
            blocks[at] = block[n]
    for high in range(2):
        parts = turn([blocks[high * 4 + n] for n in range(4)])
        for p in range(4):
            cots[p, :, 128 * high : 128 * high + 128] = parts[p]

    def run(half):
        def plane(p, carry):
            hidden = partial[p] + conv_rows(shifts, other, p, half)
            gate = 1.0 / (1.0 + jnp.exp(-hidden))
            outs[p] = (hidden * gate).astype(BF16)
            slope = gate * (1.0 + hidden * (1.0 - gate))
            grad_pre[p] = (cots[p].astype(F32) * slope).astype(BF16).reshape(2, 4, 32, 256)
            return carry

        lax.fori_loop(0, 4, plane, 0)

    by_core(core, run, 1)
    for high in range(2):
        parts = turn([outs[p, :, 128 * high : 128 * high + 128] for p in range(4)])
        for n in range(4):
            blocks[high * 4 + n] = parts[n]
    for d in range(4):
        for out, at in zip((keep, send), blocks_of(place, 1, d)):
            out[d] = blocks[at]
    for p in range(4):
        turned[:, 256 * p : 256 * p + 256] = grad_pre[p].reshape(256, 256).astype(F32).T.astype(BF16)
    by_core(core, lambda half: tap_grads(shifts, turned, given, half), 1)


def tap_grads(shifts, turned, out, half):
    for i in range(3):
        for j in range(3):
            taps = [k for k in range(3) if 13 * half <= 9 * i + 3 * j + k < 13 * half + HALF]
            if taps:
                lanes = pl.ds(256 * taps[0], 256 * len(taps))
                rhs = shifts[i : i + 4, :, 32 * j : 32 * j + 128, lanes].reshape(1024, 256 * len(taps))
                res = jnp.dot(turned[...], rhs, preferred_element_type=F32).astype(BF16)
                for n, k in enumerate(taps):
                    out[9 * i + 3 * j + k - 13 * half] = res[:, 256 * n : 256 * n + 256]


def keep_grads_body(core, shifts, turned, received, out, kept):
    by_core(core, lambda half: tap_grads(shifts, turned, kept, half))
    pack_grad_body(kept, received, out)


def weight_of(mine, other, half, tap):
    first, second = (other, mine) if half else (mine, other)
    return first[tap] if tap < HALF else second[tap - HALF]


def back_dot(rows, weight):
    return lax.dot_general(rows, weight, (((1,), (1,)), ((), ())), preferred_element_type=F32)


def input_grad_body(core, middle, before, after, mine, other, inner, edges, shifts, window):
    fill_shifts((middle, before, after, None, None), shifts, window)

    def run(half):
        def plane(p, carry):
            total = jnp.zeros((256, 256), F32)
            for i in range(3):
                for j in range(3):
                    for k in range(3):
                        lanes = pl.ds(256 * (2 - k), 256)
                        lhs = shifts[p + 2 - i, :, 32 * (2 - j) : 32 * (2 - j) + 128, lanes].reshape(256, 256)
                        total = total + back_dot(lhs, weight_of(mine, other, half, 9 * i + 3 * j + k))
            rows = total.reshape(2, 4, 32, 256)
            inner[p] = rows[:, 1:3].astype(BF16)
            edges[p, :, 0] = rows[:, 0]
            edges[p, :, 1] = rows[:, 3]
            return carry

        lax.fori_loop(0, 4, plane, 0)

    by_core(core, run)


def edge_grad_body(core, left, right, mine, other, inner, edges, out, shifts, wait):
    row = lax.broadcasted_iota(jnp.int32, (384, 256), 0) % 32
    for n, side in enumerate((left, right)):
        wide = side[...].reshape(384, 256).astype(F32)
        up = jnp.where(row == 0, 0.0, pltpu.roll(wide, 1, 0))
        down = jnp.where(row == 31, 0.0, pltpu.roll(wide, 383, 0))
        for k, part in enumerate((up, wide, down)):
            shifts[n, k] = part.astype(BF16).reshape(6, 64, 256)
    wait(0)
    out[:, :, 1:3] = inner[...]

    def run(half):
        for n, (at, j) in enumerate(((0, 2), (3, 0))):
            total = edges[:, :, n].reshape(256, 256)
            for i in range(3):
                for k in range(3):
                    lhs = shifts[n, 2 - k, 2 - i : 6 - i].reshape(256, 256)
                    total = total + back_dot(lhs, weight_of(mine, other, half, 9 * i + 3 * j + k))
            out[:, :, at] = total.astype(BF16).reshape(4, 2, 32, 256)

    by_core(core, run)


SMEM = pl.BlockSpec(memory_space=pltpu.SMEM)
FULL = pl.BlockSpec(memory_space=pltpu.VMEM)
FAR = pl.BlockSpec(memory_space=pltpu.HBM)


def local(features, kernel, filter_bias, cotangent):
    core = lax.axis_index("sample").astype(jnp.int32)
    index = core[None]
    bias = jnp.broadcast_to(filter_bias[None, None, :], (1, 32, 32))
    taps = jnp.concatenate([kernel.reshape(27, 32, 32), bias], axis=0)
    place = lax.axis_index("sy").astype(jnp.int32)[None]
    four = shape((4, 256, 128))
    blocks = call(pack_kernel_body, shape((64, 112, 128)), far_out=(0,))(index, taps)
    keep, send = call(pack_cotangent_body, (four, four))(place, cotangent)
    before, after = halo(features, "sx", 0)
    got = swap_sides(send)
    blocks, before, after, keep, got = lax.optimization_barrier((blocks, before, after, keep, got))
    blocks = lax.all_to_all(blocks, GRID, 0, 0, tiled=True)
    left, right = corners(before, features, after)
    cot = spread(keep, got)
    mine = call(unpack_kernel_body, shape((HALF, 256, 256)), far=(0,), parts=8)(blocks)
    mine, left, right, *cot = lax.optimization_barrier((mine, left, right, *cot))
    other = swap_cores(mine)
    shifts, partial = call(
        forward_first_body,
        (shape((6, 2, 192, 768)), shape((4, 256, 256), F32)),
        [pltpu.VMEM((6, 2, 192, 256), BF16)],
    )(index, features, before, after, left, right, mine)
    grad_pre, keep, send, given, turned = call(
        forward_second_body,
        (shape((4, 2, 4, 32, 256)), four, four, shape((HALF, 256, 256)), shape((256, 1024))),
        [pltpu.VMEM((8, 256, 128), BF16), pltpu.VMEM((4, 256, 256), BF16), pltpu.VMEM((4, 256, 256), BF16)],
    )(index, place, shifts, other, partial, *cot)
    before, after = halo(grad_pre, "sx", 0)
    got = swap_sides(send)
    received = swap_cores(given)
    blocks = call(
        keep_grads_body, shape((64, 112, 128)), [pltpu.VMEM((HALF, 256, 256), BF16)], far_out=(0,)
    )(index, shifts, turned, received)
    blocks, before, after, keep, got = lax.optimization_barrier((blocks, before, after, keep, got))
    left, right = corners(before, grad_pre, after)
    blocks = lax.all_to_all(blocks, GRID, 0, 0, tiled=True)
    pieces = spread(keep, got)
    half = shape((4, 2, 2, 32, 256))
    inner, edges = call(
        input_grad_body,
        (half, shape((4, 2, 2, 32, 256), F32)),
        [pltpu.VMEM((6, 2, 192, 768), BF16), pltpu.VMEM((6, 2, 192, 256), BF16)],
        far=(1, 2, 3, 4, 5),
        far_out=(0, 1),
    )(index, grad_pre, before, after, mine, other)
    blocks, inner, edges = lax.optimization_barrier((blocks, inner, edges))
    rows = call(sum_grad_body, shape((112, 128), F32))(blocks)
    rows, left, right = lax.optimization_barrier((rows, left, right))
    turned_rows = swap_cores(rows)
    input_grad = call(
        edge_grad_body,
        shape((4, 2, 4, 32, 256)),
        [pltpu.VMEM((2, 3, 6, 64, 256), BF16)],
        far=(3, 4, 5, 6),
        parts=1,
    )(index, left, right, mine, other, inner, edges)
    input_grad, *pieces = lax.optimization_barrier((input_grad, *pieces))
    output, kernel_grad = call(
        finish_body, (shape((4, 2, 32, 32, 32)), shape((27, 32, 32), F32)), far_out=(0,), parts_out=4
    )(index, place, rows, turned_rows, *pieces)
    return (output, input_grad, kernel_grad.reshape(3, 3, 3, 32, 32))


def solution(mesh):
    return jax.shard_map(
        local,
        mesh=mesh,
        in_specs=(
            P("sx", "sample", "sy", None, None),
            P(None, None, None, "sx", "sy"),
            P("sy"),
            P("sx", "sample", None, None, "sy"),
        ),
        out_specs=(
            P("sx", "sample", None, None, "sy"),
            P("sx", "sample", "sy", None, None),
            P(None, None, None, "sx", "sy"),
        ),
        check_vma=False,
    )
```
